32 devices in a mesh: proj: 8 (over z, x), lang: 4 (over y, core).
Axes of the slice: x: 2, y: 2, z: 4, core: 2. Of those that a mesh axis runs over, the one named last changes fastest.
Arguments:
- mapped_layer_arguments: bfloat16 [48, 512, 8192], P('lang', None, 'proj'), may hold values from -6 to 6
- loss_slope_at_result: bfloat16 [48, 512, 8192], P('lang', None, 'proj'), may hold values from -6 to 6
- left_lowrank_weights: bfloat16 [8192, 128], P('proj'), may hold values from -0.0625 to 0.0625
- right_lowrank_weights: bfloat16 [128, 8192], P(None, 'proj'), may hold values from -0.0625 to 0.0625
- mean_estimate_left: float32 [8192, 128], P('proj'), may hold values from -24 to 24
- variance_estimate_left: float32 [8192, 128], P('proj'), may hold values from 0.1 to 10
- mean_estimate_right: float32 [128, 8192], P(None, 'proj'), may hold values from -24 to 24
- variance_estimate_right: float32 [128, 8192], P(None, 'proj'), may hold values from 0.1 to 10
- heldout_sketched_slopes: bfloat16 [8, 256, 8192], P('lang', None, 'proj'), may hold values from -600 to 600
- tongue_label_per_example: int32 [48, 1], P('lang'), may hold values from 0 to 7; in each aligned block of 12 rows (0 to 11, 12 to 23, ...) at most 3 rows name the same one
- heldout_example_tally: int32 [8], replicated, may hold values from 1 to 256, 1280 in all
- sketch_random_key: int32 [1], replicated, may hold values from 0 to 16777215
Outputs:
- features: float32 [48, 8192], P('lang', 'proj')
- scores: float32 [48], P('lang')
The draws below stay inside these ranges and needn't reach their ends.
Inputs may be any that keep to these rules, and one draw needn't show every extreme that they name: `tongue_label_per_example`: among the 12 samples of one device, in aligned blocks of rows, no language appears more than 3 times.
All inputs are finite; a program needn't handle non-finite values.
Results may differ from the reference program's by a relative error of at most 0.0049.
Values may be sent and summed in bfloat16 or wider, within the bound.
A program may use at most 128 MiB of HBM per device.

```python
import math
import jax
import jax.numpy as jnp
import numpy as np
from jax import lax

HIDDEN_FEATURES = 8192
LOWRANK_INNER = 128
K = 8192
TOK = 512
SAMP_DEV = 12
NVAL = 256
MOST = 3
LANGS = 8
SAMPLES = 48


def draw_heldout_sketched_slopes(key, part):
    key_base, key_rows, key_cols = jax.random.split(key, 3)
    full_shape = (LANGS, NVAL, K)
    base_values = jnp.clip(jax.random.normal(key_base, full_shape, jnp.float32), -6.0, 6.0)
    row_scale = jnp.exp(jax.random.uniform(key_rows, (LANGS, NVAL, 1), jnp.float32, 0.0, math.log(10.0)))
    col_scale = jnp.exp(jax.random.uniform(key_cols, (1, 1, K), jnp.float32, 0.0, math.log(10.0)))
    return (base_values * row_scale * col_scale).astype(jnp.bfloat16)


def block_scale(rng, extent, shards, least, top_value):
    def one(position, blocks):
        heights = jax.random.uniform(jax.random.fold_in(jax.random.fold_in(rng, 6), position), (blocks,), jnp.float32, least / len(shards), top_value / len(shards))
        return jnp.repeat(jnp.exp(heights), extent[position] // blocks).reshape((-1,) + (1,) * (len(extent) - position - 1))

    factor_of = one(*shards[0])
    for cut in shards[1:]:
        factor_of = factor_of * one(*cut)
    return factor_of


def profile(amount, total, limit, lean):
    weights = [(1 << 20) // math.isqrt(grade ** lean) + 1 for grade in range(2, amount + 1)]
    spare, holding = total - limit - (amount - 1), [1] * (amount - 1)
    while spare > 0:
        candidates = [i for i in range(amount - 1) if holding[i] < limit]
        pool, remaining = sum([weights[i] for i in candidates]), spare
        for i in candidates:
            extra = min(limit - holding[i], max(1, remaining * weights[i] // pool), spare)
            holding[i] = holding[i] + extra
            spare = spare - extra
    return np.array([limit] + holding)


def uneven_parts(key, count, total, limit, lean):
    if count == 2:
        one = jax.random.randint(key, (), max(1, total - limit), min(limit, total - 1) + 1)
        return jnp.stack([one, total - one])
    lengths = jnp.asarray(profile(count, total, limit, lean), jnp.int32)
    couples = (count - 1) // 2
    giver, sink = lengths[1:1 + 2 * couples:2], lengths[2:2 + 2 * couples:2]
    slack = jnp.minimum(giver - 1, limit - sink)
    shifted = jax.random.randint(jax.random.fold_in(key, 1), (couples,), 0, 1 << 20) % (slack + 1)
    lengths = lengths.at[1:1 + 2 * couples:2].set(giver - shifted).at[2:2 + 2 * couples:2].set(sink + shifted)
    return lengths[jax.random.permutation(jax.random.fold_in(key, 2), count)]


def assign_block(stream_key, own, number, rows, number_of, top, reach, skew):
    sequence = jax.random.permutation(stream_key, number_of)
    crowded, ordinary = load_shares(number_of, rows * top, reach, skew, True), load_shares(number_of, rows * top, reach, skew, False)
    places = jnp.arange(number_of)

    def named(sizes, offset_by):
        used = int((sizes > 0).sum())
        fixed = max(1, used // 4)
        passed = fixed + (places - fixed + offset_by * (used - fixed)) % max(1, number_of - fixed)
        return jnp.zeros((number_of,), jnp.int32).at[sequence[jnp.where(places < fixed, places, passed)]].set(jnp.asarray(sizes, jnp.int32))

    sizes = jnp.where(number % 4 == 0, named(crowded, number // 4), named(ordinary, number - number // 4 - 1))
    mixed = jax.random.permutation(jax.random.fold_in(own, 3), number_of)
    source_of, sink = mixed[0:number_of // 2 * 2:2], mixed[1:number_of // 2 * 2:2]
    room = jnp.minimum(sizes[source_of] - 1, reach - sizes[sink]) // 2
    room = jnp.where((source_of == sequence[0]) | (sink == sequence[0]) | (sizes[sink] == 0), 0, jnp.maximum(room, 0))
    passed = jax.random.randint(jax.random.fold_in(own, 4), (number_of // 2,), 0, 1 << 20) % (room + 1)
    sizes = sizes.at[source_of].add(-passed).at[sink].add(passed)
    items = jnp.searchsorted(jnp.cumsum(sizes), jnp.arange(rows * top), side="right").astype(jnp.int32)
    grid = items.reshape(top, rows).T
    grid = grid[jax.random.permutation(jax.random.fold_in(own, 1), rows)]
    offset_by = jax.random.randint(jax.random.fold_in(own, 2), (rows, 1), 0, top)
    return jnp.take_along_axis(grid, (jnp.arange(top)[None, :] + offset_by) % top, axis=1)


def load_shares(number_of, total, reach, skew, full):
    weights = [(1 << 20) // math.isqrt(rank ** skew) + 1 for rank in range(1, number_of + 1)]
    largest = reach if full else min(reach, max(-(-total // number_of), total * weights[0] // sum(weights)))
    least = 1 if total - largest >= number_of - 1 else 0
    counts, surplus = [largest] + [least] * (number_of - 1), total - largest - least * (number_of - 1)
    while surplus > 0:
        movable = [i for i in range(1, number_of) if counts[i] < largest] or [i for i in range(1, number_of) if counts[i] < reach]
        mass, budget = sum([weights[i] for i in movable]), surplus
        for i in movable:
            more = min(reach - counts[i], max(1, budget * weights[i] // mass), surplus)
            counts[i] = counts[i] + more
            surplus = surplus - more
    return np.array(counts)


def gaussian(own_key, shape, scale, most, pieces=(), held_as=jnp.bfloat16):
    values = scale * jax.random.normal(own_key, shape, jnp.float32)
    if pieces:
        values = values * block_scale(own_key, shape, pieces, -0.22, 0.18)
    return jnp.clip(values, -most, most).astype(held_as)


def setup_inputs(seed: int = 0) -> dict:
    key_list = jax.random.split(jax.random.key(seed), 13)
    mapped_layer_arguments = gaussian(key_list[0], (SAMPLES, TOK, HIDDEN_FEATURES), 1.0, 6.0, ((0, 4), (2, 8)))
    loss_slope_at_result = gaussian(key_list[1], (SAMPLES, TOK, HIDDEN_FEATURES), 1.0, 6.0, ((0, 4), (2, 8)))
    left_lowrank_weights = gaussian(key_list[2], (HIDDEN_FEATURES, LOWRANK_INNER), HIDDEN_FEATURES ** -0.5, 0.0625, ((0, 8),))
    right_lowrank_weights = gaussian(key_list[3], (LOWRANK_INNER, HIDDEN_FEATURES), HIDDEN_FEATURES ** -0.5, 0.0625, ((1, 8),))
    mean_estimate_left = gaussian(key_list[4], (HIDDEN_FEATURES, LOWRANK_INNER), 4.0, 24.0, ((0, 8),), jnp.float32)
    variance_estimate_left = jnp.clip(jnp.exp(math.log(10.0) - 4.6051702 * jax.random.uniform(key_list[5], (HIDDEN_FEATURES, LOWRANK_INNER), jnp.float32) ** block_scale(key_list[5], (HIDDEN_FEATURES, LOWRANK_INNER), ((0, 8),), -0.2, 0.2)), 0.1, 10.0)
    mean_estimate_right = gaussian(key_list[6], (LOWRANK_INNER, HIDDEN_FEATURES), 4.0, 24.0, ((1, 8),), jnp.float32)
    variance_estimate_right = jnp.clip(jnp.exp(math.log(10.0) - 4.6051702 * jax.random.uniform(key_list[7], (LOWRANK_INNER, HIDDEN_FEATURES), jnp.float32) ** block_scale(key_list[7], (LOWRANK_INNER, HIDDEN_FEATURES), ((1, 8),), -0.2, 0.2)), 0.1, 10.0)
    heldout_sketched_slopes = draw_heldout_sketched_slopes(jax.random.fold_in(key_list[12], 71), 0)
    tongue_label_per_example_keys = jax.random.split(jax.random.fold_in(key_list[9], 1), SAMPLES // SAMP_DEV)
    tongue_label_per_example_turns = jax.random.permutation(jax.random.fold_in(key_list[9], 3), SAMPLES // SAMP_DEV)
    tongue_label_per_example = jax.vmap(lambda own, number: assign_block(jax.random.fold_in(key_list[9], 2), own, number, SAMP_DEV, LANGS, 1, MOST, 2))(tongue_label_per_example_keys, tongue_label_per_example_turns).reshape((SAMPLES, 1))
    heldout_example_tally = uneven_parts(key_list[10], LANGS, 5 * NVAL, NVAL, 2).astype(jnp.int32)
    sketch_random_key = jax.random.randint(key_list[11], (1,), 0, 16777216).astype(jnp.int32)
    return {"mapped_layer_arguments": mapped_layer_arguments, "loss_slope_at_result": loss_slope_at_result, "left_lowrank_weights": left_lowrank_weights, "right_lowrank_weights": right_lowrank_weights, "mean_estimate_left": mean_estimate_left, "variance_estimate_left": variance_estimate_left, "mean_estimate_right": mean_estimate_right, "variance_estimate_right": variance_estimate_right, "heldout_sketched_slopes": heldout_sketched_slopes, "tongue_label_per_example": tongue_label_per_example, "heldout_example_tally": heldout_example_tally, "sketch_random_key": sketch_random_key}


update_multiplier = 1.25

def scramble(hashed):
    hashed = jnp.bitwise_xor(hashed, lax.shift_right_logical(hashed, jnp.int32(16)))
    hashed = hashed * 2146121005
    hashed = jnp.bitwise_xor(hashed, lax.shift_right_logical(hashed, jnp.int32(15)))
    hashed = hashed * 739982445
    hashed = jnp.bitwise_xor(hashed, lax.shift_right_logical(hashed, jnp.int32(16)))
    return hashed

def sign_table(seed_value, table_id, row_count, row_start, col_count):
    row_ids = (row_start + lax.iota(jnp.int32, row_count)).astype(jnp.int32)
    col_ids = lax.iota(jnp.int32, col_count)
    anchor = scramble((seed_value * 4 + table_id).astype(jnp.int32))
    hashed = scramble(anchor + row_ids[:, None] * col_count + col_ids[None, :])
    sign_bit = jnp.bitwise_and(lax.shift_right_logical(hashed, jnp.int32(13)), 1)
    return (1 - 2 * sign_bit).astype(jnp.float32)

def precondition(gradient, moment, second):
    return ((0.9 * moment + 0.1 * gradient) * lax.rsqrt(0.999 * second + 0.001 * gradient * gradient)).astype(jnp.bfloat16)

def reference(mapped_layer_arguments, loss_slope_at_result, left_lowrank_weights, right_lowrank_weights, mean_estimate_left, variance_estimate_left, mean_estimate_right, variance_estimate_right, heldout_sketched_slopes, tongue_label_per_example, heldout_example_tally, sketch_random_key):
    seed_value = sketch_random_key[0].astype(jnp.int32)
    anchor_row = jnp.int32(0)
    up_left = sign_table(seed_value, 0, LOWRANK_INNER, anchor_row, K)
    up_right = sign_table(seed_value, 1, HIDDEN_FEATURES, anchor_row, K)
    down_left = sign_table(seed_value, 2, HIDDEN_FEATURES, anchor_row, K)
    down_right = sign_table(seed_value, 3, LOWRANK_INNER, anchor_row, K)

    def one_sample(sample_pair):
        entering_signals, output_slope_gathered = sample_pair
        entering_signal_accumulated = (update_multiplier * jnp.dot(entering_signals, left_lowrank_weights, preferred_element_type=jnp.float32)).astype(jnp.bfloat16)
        output_slope_accumulated = (update_multiplier * jnp.dot(output_slope_gathered, right_lowrank_weights.T, preferred_element_type=jnp.float32)).astype(jnp.bfloat16)
        grad_up = jnp.dot(entering_signal_accumulated.T, output_slope_gathered, preferred_element_type=jnp.float32)
        grad_down = jnp.dot(entering_signals.T, output_slope_accumulated, preferred_element_type=jnp.float32)
        step_up = precondition(grad_up, mean_estimate_right, variance_estimate_right)
        step_down = precondition(grad_down, mean_estimate_left, variance_estimate_left)
        mixed_up = jnp.dot(step_up.astype(jnp.float32), up_right, precision=lax.Precision.HIGHEST)
        mixed_down = jnp.dot(step_down.T.astype(jnp.float32), down_left, precision=lax.Precision.HIGHEST)
        return lax.optimization_barrier(jnp.sum(mixed_up * up_left + mixed_down * down_right, axis=0))
    projected = lax.map(one_sample, (mapped_layer_arguments, loss_slope_at_result))
    features = projected * lax.rsqrt(lax.optimization_barrier(jnp.mean(projected * projected, axis=-1, keepdims=True)) + 1e-06)
    feat_low = features.astype(jnp.bfloat16)
    val_wide = heldout_sketched_slopes.astype(jnp.float32)
    val_rms = jnp.sqrt(lax.optimization_barrier(jnp.mean(val_wide * val_wide, axis=-1)) + 1e-06)
    lang_of = tongue_label_per_example[:, 0].astype(jnp.int32)
    flat_val = heldout_sketched_slopes.reshape(LANGS * NVAL, K)
    dot_sums = jnp.dot(feat_low, flat_val.T, preferred_element_type=jnp.float32).reshape(SAMPLES, LANGS, NVAL)
    similar = dot_sums / (math.sqrt(K) * val_rms[None, :, :])
    own_sim = jnp.take_along_axis(similar, lang_of[:, None, None], axis=1)[:, 0, :]
    own_count = heldout_example_tally[lang_of]
    is_valid = lax.iota(jnp.int32, NVAL)[None, :] < own_count[:, None]
    scores = lax.optimization_barrier(jnp.max(jnp.where(is_valid, own_sim, jnp.float32(-1e+30)), axis=-1))
    return (features, scores)
```

```python
import functools
import math

import jax
import jax.numpy as jnp
from jax import lax
from jax.experimental import pallas as pl
from jax.experimental.pallas import tpu as pltpu
from jax.sharding import PartitionSpec as P

RANK = 128
UPDATE_MULTIPLIER = 1.25
M1 = 2146121005
M2_UP = (739982445 * 4 + 2**31) % 2**32 - 2**31


def scramble(hashed):
    hashed = jnp.bitwise_xor(hashed, lax.shift_right_logical(hashed, jnp.int32(16)))
    hashed = hashed * 2146121005
    hashed = jnp.bitwise_xor(hashed, lax.shift_right_logical(hashed, jnp.int32(15)))
    hashed = hashed * 739982445
    hashed = jnp.bitwise_xor(hashed, lax.shift_right_logical(hashed, jnp.int32(16)))
    return hashed


def table_kernel(cols, base_ref, out_ref):
    rows, width = out_ref.shape
    step, piece = 16, 512
    base = base_ref[pl.program_id(0)] + pl.program_id(1) * width
    local = lax.broadcasted_iota(jnp.int32, (step, piece), 0) * cols + lax.broadcasted_iota(
        jnp.int32, (step, piece), 1
    )

    def one(i, carry):
        for j in range(width // piece):
            h = local + (base + i * (step * cols) + j * piece)
            h = h ^ lax.shift_right_logical(h, jnp.int32(16))
            h = h * jnp.int32(M1)
            h = h ^ lax.shift_right_logical(h, jnp.int32(15))
            h = h * jnp.int32(M2_UP)
            h = h ^ lax.shift_left(h, jnp.int32(16))
            sign = jnp.where(h < 0, jnp.float32(-1.0), jnp.float32(1.0))
            out_ref[pl.ds(pl.multiple_of(i * step, step), step), j * piece : (j + 1) * piece] = (
                sign.astype(jnp.bfloat16)
            )
        return carry

    lax.fori_loop(0, rows // step, one, 0)


def sign_tables(bases, cols):
    blocks = bases.shape[0]
    width = 2048
    return pl.pallas_call(
        functools.partial(table_kernel, cols),
        grid=(blocks, cols // width),
        in_specs=[pl.BlockSpec(memory_space=pltpu.SMEM)],
        out_specs=pl.BlockSpec((128, width), lambda i, j: (i, j)),
        out_shape=jax.ShapeDtypeStruct((blocks * 128, cols), jnp.bfloat16),
        cost_estimate=pl.CostEstimate(
            flops=blocks * 128 * cols * 12, bytes_accessed=blocks * 256 * cols, transcendentals=0
        ),
        name="sign_tables",
    )(bases)


def step_kernel(x_ref, g_ref, lx_ref, lg_ref, ml_ref, vl_ref, mr_ref, vr_ref, up_ref, dn_ref):
    def one(low, wide, moment, second, out):
        grad = lax.dot_general(
            low[0], wide[0], (((0,), (0,)), ((), ())), preferred_element_type=jnp.float32
        )
        out[...] = (
            (0.9 * moment[...] + 0.1 * grad)
            * lax.rsqrt(0.999 * second[...] + 0.001 * grad * grad)
        ).astype(jnp.bfloat16)

    one(lx_ref, g_ref, mr_ref, vr_ref, up_ref)
    one(lg_ref, x_ref, ml_ref, vl_ref, dn_ref)


def steps(x, g, lx, lg, ml_t, vl_t, mr, vr):
    n, tok, w = x.shape
    wide = pl.BlockSpec((1, tok, w), lambda i: (i, 0, 0))
    low = pl.BlockSpec((1, tok, RANK), lambda i: (i, 0, 0))
    whole = pl.BlockSpec((RANK, w), lambda i: (0, 0))
    out = pl.BlockSpec((RANK, w), lambda i: (i, 0))
    return pl.pallas_call(
        step_kernel,
        grid=(n,),
        in_specs=[wide, wide, low, low, whole, whole, whole, whole],
        out_specs=[out, out],
        out_shape=[jax.ShapeDtypeStruct((n * RANK, w), jnp.bfloat16)] * 2,
        cost_estimate=pl.CostEstimate(
            flops=n * tok * w * RANK * 4, bytes_accessed=n * tok * w * 4, transcendentals=0
        ),
        compiler_params=pltpu.CompilerParams(vmem_limit_bytes=48 * 1024 * 1024),
        name="adam_steps",
    )(x, g, lx, lg, ml_t, vl_t, mr, vr)


def project_kernel(up_ref, dn_ref, tu_ref, td_ref, ul_ref, dr_ref, out_ref):
    n = up_ref.shape[0] // RANK
    mixed_up = jnp.dot(up_ref[...], tu_ref[...], preferred_element_type=jnp.float32)
    mixed_dn = jnp.dot(dn_ref[...], td_ref[...], preferred_element_type=jnp.float32)
    ul = ul_ref[...].astype(jnp.float32)
    dr = dr_ref[...].astype(jnp.float32)
    for i in range(n):
        part = slice(i * RANK, (i + 1) * RANK)
        out_ref[i : i + 1, :] = jnp.sum(
            mixed_up[part] * ul + mixed_dn[part] * dr, axis=0, keepdims=True
        )


def project(up, dn, tables):
    rows, w = up.shape
    n = rows // RANK
    cols = tables.shape[1]
    tile = 256
    edge = 2 * w // RANK
    whole = pl.BlockSpec((rows, w), lambda k: (0, 0))
    return pl.pallas_call(
        project_kernel,
        grid=(cols // tile,),
        in_specs=[
            whole,
            whole,
            pl.BlockSpec((w, tile), lambda k: (0, k)),
            pl.BlockSpec((w, tile), lambda k: (1, k)),
            pl.BlockSpec((RANK, tile), lambda k: (edge, k)),
            pl.BlockSpec((RANK, tile), lambda k: (edge + 1, k)),
        ],
        out_specs=pl.BlockSpec((n, tile), lambda k: (0, k)),
        out_shape=jax.ShapeDtypeStruct((n, cols), jnp.float32),
        cost_estimate=pl.CostEstimate(
            flops=4 * rows * w * cols, bytes_accessed=4 * w * cols + 4 * rows * w, transcendentals=0
        ),
        compiler_params=pltpu.CompilerParams(vmem_limit_bytes=48 * 1024 * 1024),
        name="project",
    )(up, dn, tables, tables, tables, tables)


def per_device(
    mapped_layer_arguments,
    loss_slope_at_result,
    left_lowrank_weights,
    right_lowrank_weights,
    mean_estimate_left,
    variance_estimate_left,
    mean_estimate_right,
    variance_estimate_right,
    heldout_sketched_slopes,
    tongue_label_per_example,
    heldout_example_tally,
    sketch_random_key,
):
    shard_id = lax.axis_index("proj")
    shards = lax.axis_size("proj")
    n, tok, w = mapped_layer_arguments.shape
    K = w * shards
    nval = heldout_sketched_slopes.shape[1]

    part_in = jnp.einsum(
        "ntw,wr->ntr", mapped_layer_arguments, left_lowrank_weights,
        preferred_element_type=jnp.float32,
    ).astype(jnp.bfloat16)
    part_gr = jnp.einsum(
        "ntw,rw->ntr", loss_slope_at_result, right_lowrank_weights,
        preferred_element_type=jnp.float32,
    ).astype(jnp.bfloat16)
    parts = jnp.stack([part_in, part_gr]).reshape(2, n * tok, RANK)
    share = lax.psum_scatter(parts, "proj", scatter_dimension=1, tiled=True)
    share = (UPDATE_MULTIPLIER * share.astype(jnp.float32)).astype(jnp.bfloat16)
    low = lax.all_gather(share, "proj", axis=1, tiled=True).reshape(2, n, tok, RANK)

    seed4 = sketch_random_key[0] * 4
    inner = jnp.arange(w // RANK, dtype=jnp.int32) * (RANK * K) + shard_id * (w * K)
    bases = jnp.concatenate([
        scramble(seed4 + 1) + inner,
        scramble(seed4 + 2) + inner,
        scramble(seed4)[None],
        scramble(seed4 + 3)[None],
    ])
    tables = sign_tables(bases, K)

    up, dn = steps(
        mapped_layer_arguments, loss_slope_at_result, low[0], low[1],
        mean_estimate_left.T, variance_estimate_left.T, mean_estimate_right, variance_estimate_right,
    )
    projected = project(up, dn, tables)

    all_val = lax.all_gather(heldout_sketched_slopes, "lang", axis=0, tiled=True)
    val_wide = all_val.astype(jnp.float32)
    val_square = lax.psum(jnp.sum(val_wide * val_wide, axis=-1), "proj")

    raw = lax.psum_scatter(projected, "proj", scatter_dimension=1, tiled=True)
    lang_of = tongue_label_per_example[:, 0]
    num_langs = heldout_example_tally.shape[0]
    one_hot = (lang_of[:, None] == lax.iota(jnp.int32, num_langs)[None, :]).astype(jnp.float32)
    partial_all = jnp.einsum(
        "nc,ljc->nlj", raw.astype(jnp.bfloat16), all_val, preferred_element_type=jnp.float32
    )
    own_part = jnp.sum(partial_all * one_hot[:, :, None], axis=1)
    own_square = jnp.sum(raw * raw, axis=-1, keepdims=True)
    sums = lax.psum(jnp.concatenate([own_part, jnp.broadcast_to(own_square, (n, RANK))], axis=1), "proj")
    inverse = lax.rsqrt(sums[:, nval : nval + 1] / K + 1e-06)
    features = raw * inverse
    rms_all = jnp.sqrt(val_square / K + 1e-06)
    rms_own = jnp.sum(one_hot[:, :, None] * rms_all[None, :, :], axis=1)
    count_own = jnp.sum(one_hot.astype(jnp.int32) * heldout_example_tally[None, :], axis=1)
    similar = sums[:, :nval] * inverse / (math.sqrt(K) * rms_own)
    is_valid = lax.iota(jnp.int32, nval)[None, :] < count_own[:, None]
    scores = jnp.max(jnp.where(is_valid, similar, jnp.float32(-1e30)), axis=-1)
    return (features, scores)


def solution(mesh):
    in_specs = (
        P("lang", None, "proj"),
        P("lang", None, "proj"),
        P("proj", None),
        P(None, "proj"),
        P("proj", None),
        P("proj", None),
        P(None, "proj"),
        P(None, "proj"),
        P("lang", None, "proj"),
        P("lang", None),
        P(),
        P(),
    )
    out_specs = (P("lang", "proj"), P("lang"))
    return jax.shard_map(
        per_device, mesh=mesh, in_specs=in_specs, out_specs=out_specs, check_vma=False
    )
```

```python
import functools
import math

import jax
import jax.numpy as jnp
from jax import lax
from jax.experimental import pallas as pl
from jax.experimental.pallas import tpu as pltpu
from jax.sharding import PartitionSpec as P

RANK = 128
UPDATE_MULTIPLIER = 1.25
M1 = 2146121005
M2_UP = (739982445 * 4 + 2**31) % 2**32 - 2**31


def scramble(hashed):
    hashed = jnp.bitwise_xor(hashed, lax.shift_right_logical(hashed, jnp.int32(16)))
    hashed = hashed * 2146121005
    hashed = jnp.bitwise_xor(hashed, lax.shift_right_logical(hashed, jnp.int32(15)))
    hashed = hashed * 739982445
    hashed = jnp.bitwise_xor(hashed, lax.shift_right_logical(hashed, jnp.int32(16)))
    return hashed


def table_kernel(cols, base_ref, out_ref):
    rows, width = out_ref.shape
    step, piece = 16, 512
    base = base_ref[pl.program_id(0)] + pl.program_id(1) * width
    local = lax.broadcasted_iota(jnp.int32, (step, piece), 0) * cols + lax.broadcasted_iota(
        jnp.int32, (step, piece), 1
    )

    def one(i, carry):
        for j in range(width // piece):
            h = local + (base + i * (step * cols) + j * piece)
            h = h ^ lax.shift_right_logical(h, jnp.int32(16))
            h = h * jnp.int32(M1)
            h = h ^ lax.shift_right_logical(h, jnp.int32(15))
            h = h * jnp.int32(M2_UP)
            h = h ^ lax.shift_left(h, jnp.int32(16))
            sign = jnp.where(h < 0, jnp.float32(-1.0), jnp.float32(1.0))
            out_ref[pl.ds(pl.multiple_of(i * step, step), step), j * piece : (j + 1) * piece] = (
                sign.astype(jnp.bfloat16)
            )
        return carry

    lax.fori_loop(0, rows // step, one, 0)


def sign_tables(bases, cols):
    blocks = bases.shape[0]
    width = 2048
    return pl.pallas_call(
        functools.partial(table_kernel, cols),
        grid=(blocks, cols // width),
        in_specs=[pl.BlockSpec(memory_space=pltpu.SMEM)],
        out_specs=pl.BlockSpec((128, width), lambda i, j: (i, j)),
        out_shape=jax.ShapeDtypeStruct((blocks * 128, cols), jnp.bfloat16),
        cost_estimate=pl.CostEstimate(
            flops=blocks * 128 * cols * 12, bytes_accessed=blocks * 256 * cols, transcendentals=0
        ),
        name="sign_tables",
    )(bases)


def share_kernel(pieces_ref, order_ref, out_ref):
    total = pieces_ref[0].astype(jnp.float32)
    for i in range(1, pieces_ref.shape[0]):
        total = total + pieces_ref[i].astype(jnp.float32)
    out_ref[...] = (UPDATE_MULTIPLIER * total).astype(jnp.bfloat16)


def share_of(pieces, after, name):
    _, rows, rank = pieces.shape
    vmem = pl.BlockSpec(memory_space=pltpu.VMEM)
    return pl.pallas_call(
        share_kernel,
        in_specs=[vmem, pl.BlockSpec(memory_space=pl.ANY)],
        out_specs=vmem,
        out_shape=jax.ShapeDtypeStruct((rows, rank), jnp.bfloat16),
        compiler_params=pltpu.CompilerParams(vmem_limit_bytes=16 * 1024 * 1024),
        name=name,
    )(pieces, after)


def step_kernel(wide_ref, low_ref, moment_ref, second_ref, order_ref, out_ref):
    grad = lax.dot_general(
        low_ref[0], wide_ref[0], (((0,), (0,)), ((), ())), preferred_element_type=jnp.float32
    )
    out_ref[...] = (
        (0.9 * moment_ref[...] + 0.1 * grad)
        * lax.rsqrt(0.999 * second_ref[...] + 0.001 * grad * grad)
    ).astype(jnp.bfloat16)


def steps(wide, low, moment, second, after, name):
    n, tok, w = wide.shape
    whole = pl.BlockSpec((RANK, w), lambda i: (0, 0))
    return pl.pallas_call(
        step_kernel,
        grid=(n,),
        in_specs=[
            pl.BlockSpec((1, tok, w), lambda i: (i, 0, 0)),
            pl.BlockSpec((1, tok, RANK), lambda i: (i, 0, 0)),
            whole,
            whole,
            pl.BlockSpec(memory_space=pl.ANY),
        ],
        out_specs=pl.BlockSpec((RANK, w), lambda i: (i, 0)),
        out_shape=jax.ShapeDtypeStruct((n * RANK, w), jnp.bfloat16),
        cost_estimate=pl.CostEstimate(
            flops=n * tok * w * RANK * 2, bytes_accessed=n * tok * w * 2, transcendentals=0
        ),
        compiler_params=pltpu.CompilerParams(vmem_limit_bytes=32 * 1024 * 1024),
        name=name,
    )(wide, low, moment, second, after)


def project_kernel(has_prior, *refs):
    if has_prior:
        step_ref, table_ref, side_ref, prior_ref, out_ref = refs
    else:
        step_ref, table_ref, side_ref, out_ref = refs
    n = step_ref.shape[0] // RANK
    mixed = jnp.dot(step_ref[...], table_ref[...], preferred_element_type=jnp.float32)
    side = side_ref[...].astype(jnp.float32)
    for i in range(n):
        row = jnp.sum(mixed[i * RANK : (i + 1) * RANK] * side, axis=0, keepdims=True)
        if has_prior:
            row = row + prior_ref[i : i + 1, :]
        out_ref[i : i + 1, :] = row


def project(step, tables, name, prior):
    rows, w = step.shape
    n = rows // RANK
    cols = tables.shape[1]
    tile = min(512, w)
    inner = w // tile
    edge = w // RANK
    out = pl.BlockSpec((None, n, tile), lambda k: (k // inner, 0, k % inner))
    in_specs = [
        pl.BlockSpec((rows, w), lambda k: (0, 0)),
        pl.BlockSpec((w, tile), lambda k: (0, k)),
        pl.BlockSpec((RANK, tile), lambda k: (edge, k)),
    ]
    operands = [step, tables, tables]
    if prior is not None:
        in_specs.append(out)
        operands.append(prior)
    return pl.pallas_call(
        functools.partial(project_kernel, prior is not None),
        grid=(cols // tile,),
        in_specs=in_specs,
        out_specs=out,
        out_shape=jax.ShapeDtypeStruct((cols // w, n, w), jnp.float32),
        cost_estimate=pl.CostEstimate(
            flops=2 * rows * w * cols, bytes_accessed=2 * w * cols + 2 * rows * w, transcendentals=0
        ),
        compiler_params=pltpu.CompilerParams(vmem_limit_bytes=40 * 1024 * 1024),
        name=name,
    )(*operands)


def finish_kernel(
    shards, langs, nval,
    proj_ref, val_ref, hot_ref, square_ref, count_ref,
    feat_ref, score_ref,
    land, message, notes, send1, recv1, send2, recv2,
):
    me = lax.axis_index("proj")
    n, w = feat_ref.shape
    cols = shards * w
    barrier = pltpu.get_barrier_semaphore()
    for d in range(1, shards):
        pl.semaphore_signal(
            barrier, inc=1, device_id={"proj": lax.rem(me + d, shards)},
            device_id_type=pl.DeviceIdType.MESH,
        )
    pl.semaphore_wait(barrier, shards - 1)

    first = []
    for d in range(1, shards):
        target = lax.rem(me + d, shards)
        copy = pltpu.make_async_remote_copy(
            src_ref=proj_ref.at[target], dst_ref=land.at[d - 1],
            send_sem=send1.at[d - 1], recv_sem=recv1.at[d - 1],
            device_id={"proj": target}, device_id_type=pl.DeviceIdType.MESH,
        )
        copy.start()
        first.append(copy)
    message[n:, :] = jnp.zeros((message.shape[0] - n, message.shape[1]), jnp.float32)
    message[16 : 16 + n, :nval] = square_ref[...]
    raw = proj_ref[me]
    for copy in first:
        copy.wait_recv()
    for d in range(1, shards):
        raw = raw + land[d - 1]
    dots = lax.dot_general(
        raw.astype(jnp.bfloat16), val_ref[...], (((1,), (1,)), ((), ())),
        preferred_element_type=jnp.float32,
    )
    own = jnp.zeros((n, nval), jnp.float32)
    for l in range(langs):
        own = own + hot_ref[:, l : l + 1] * dots[:, l * nval : (l + 1) * nval]
    message[:n, :nval] = own
    message[:n, nval:] = jnp.broadcast_to(
        jnp.sum(raw * raw, axis=1, keepdims=True), (n, message.shape[1] - nval)
    )
    second = []
    for d in range(1, shards):
        target = lax.rem(me + d, shards)
        copy = pltpu.make_async_remote_copy(
            src_ref=message, dst_ref=notes.at[d - 1],
            send_sem=send2.at[d - 1], recv_sem=recv2.at[d - 1],
            device_id={"proj": target}, device_id_type=pl.DeviceIdType.MESH,
        )
        copy.start()
        second.append(copy)
    total = message[...]
    for copy in second:
        copy.wait_recv()
    for d in range(1, shards):
        total = total + notes[d - 1]
    inverse = lax.rsqrt(total[:n, nval : nval + 1] / cols + 1e-06)
    feat_ref[...] = raw * inverse
    rms = jnp.sqrt(total[16 : 16 + n, :nval] / cols + 1e-06)
    similar = total[:n, :nval] * inverse / (math.sqrt(cols) * rms)
    live = lax.broadcasted_iota(jnp.int32, (n, nval), 1) < count_ref[...]
    best = jnp.max(jnp.where(live, similar, jnp.float32(-1e30)), axis=1, keepdims=True)
    score_ref[...] = jnp.broadcast_to(best, score_ref.shape)
    for copy in first + second:
        copy.wait_send()


def finish(projected, all_val, hot, own_square, count):
    shards, n, w = projected.shape
    langs, nval = all_val.shape[0], all_val.shape[1]
    vmem = pl.BlockSpec(memory_space=pltpu.VMEM)
    return pl.pallas_call(
        functools.partial(finish_kernel, shards, langs, nval),
        in_specs=[vmem] * 5,
        out_specs=[vmem] * 2,
        out_shape=[
            jax.ShapeDtypeStruct((n, w), jnp.float32),
            jax.ShapeDtypeStruct((n, 128), jnp.float32),
        ],
        scratch_shapes=[
            pltpu.VMEM((shards - 1, n, w), jnp.float32),
            pltpu.VMEM((32, nval + 128), jnp.float32),
            pltpu.VMEM((shards - 1, 32, nval + 128), jnp.float32),
            pltpu.SemaphoreType.DMA((shards - 1,)),
            pltpu.SemaphoreType.DMA((shards - 1,)),
            pltpu.SemaphoreType.DMA((shards - 1,)),
            pltpu.SemaphoreType.DMA((shards - 1,)),
        ],
        compiler_params=pltpu.CompilerParams(
            collective_id=0, has_side_effects=True, vmem_limit_bytes=32 * 1024 * 1024
        ),
        name="finish",
    )(projected, all_val.reshape(langs * nval, w), hot, own_square, count)


def per_device(
    mapped_layer_arguments,
    loss_slope_at_result,
    left_lowrank_weights,
    right_lowrank_weights,
    mean_estimate_left,
    variance_estimate_left,
    mean_estimate_right,
    variance_estimate_right,
    heldout_sketched_slopes,
    tongue_label_per_example,
    heldout_example_tally,
    sketch_random_key,
):
    shard_id = lax.axis_index("proj")
    shards = lax.axis_size("proj")
    n, tok, w = mapped_layer_arguments.shape
    K = w * shards

    part_in = jnp.einsum(
        "ntw,wr->ntr", mapped_layer_arguments, left_lowrank_weights,
        preferred_element_type=jnp.float32,
    ).astype(jnp.bfloat16)
    part_gr = jnp.einsum(
        "ntw,rw->ntr", loss_slope_at_result, right_lowrank_weights,
        preferred_element_type=jnp.float32,
    ).astype(jnp.bfloat16)

    def pieces_of(part):
        return lax.all_to_all(
            part.reshape(shards, n * tok // shards, RANK), "proj", split_axis=0, concat_axis=0
        )

    def gather(share):
        return lax.all_gather(share, "proj", axis=0, tiled=True).reshape(n, tok, RANK)

    seed4 = sketch_random_key[0] * 4
    inner = jnp.arange(w // RANK, dtype=jnp.int32) * (RANK * K) + shard_id * (w * K)
    tables = [
        sign_tables(
            jnp.concatenate([scramble(seed4 + wide) + inner, scramble(seed4 + narrow)[None]]), K
        )
        for wide, narrow in ((1, 0), (2, 3))
    ]
    low_in = gather(share_of(pieces_of(part_in), tables[0], "share_in"))
    low_gr = gather(share_of(pieces_of(part_gr), tables[1], "share_gr"))

    up = steps(
        loss_slope_at_result, low_in, mean_estimate_right, variance_estimate_right, tables[1],
        "steps_up"
    )
    half = project(up, tables[0], "project_up", None)
    dn = steps(
        mapped_layer_arguments, low_gr, mean_estimate_left.T, variance_estimate_left.T, half,
        "steps_down"
    )
    projected = project(dn, tables[1], "project_down", half)

    all_val = lax.all_gather(heldout_sketched_slopes, "lang", axis=0, tiled=True)
    val_wide = all_val.astype(jnp.float32)
    val_square = jnp.sum(val_wide * val_wide, axis=-1)
    lang_of = tongue_label_per_example[:, 0]
    num_langs = heldout_example_tally.shape[0]
    hot = (lang_of[:, None] == lax.iota(jnp.int32, num_langs)[None, :]).astype(jnp.float32)
    own_square = jnp.sum(hot[:, :, None] * val_square[None, :, :], axis=1)
    count_own = jnp.sum(
        hot.astype(jnp.int32) * heldout_example_tally[None, :], axis=1, keepdims=True
    )
    features, scores = finish(projected, all_val, hot, own_square, count_own)
    scores = scores[:, 0]
    return (features, scores)


def solution(mesh):
    in_specs = (
        P("lang", None, "proj"),
        P("lang", None, "proj"),
        P("proj", None),
        P(None, "proj"),
        P("proj", None),
        P("proj", None),
        P(None, "proj"),
        P(None, "proj"),
        P("lang", None, "proj"),
        P("lang", None),
        P(),
        P(),
    )
    out_specs = (P("lang", "proj"), P("lang"))
    return jax.shard_map(
        per_device, mesh=mesh, in_specs=in_specs, out_specs=out_specs, check_vma=False
    )
```

```python
import functools
import math

import jax
import jax.numpy as jnp
from jax import lax
from jax.experimental import pallas as pl
from jax.experimental.pallas import tpu as pltpu
from jax.sharding import PartitionSpec as P

RANK = 128
UPDATE_MULTIPLIER = 1.25
M1 = 2146121005
M2_UP = (739982445 * 4 + 2**31) % 2**32 - 2**31


def scramble(hashed):
    hashed = jnp.bitwise_xor(hashed, lax.shift_right_logical(hashed, jnp.int32(16)))
    hashed = hashed * 2146121005
    hashed = jnp.bitwise_xor(hashed, lax.shift_right_logical(hashed, jnp.int32(15)))
    hashed = hashed * 739982445
    hashed = jnp.bitwise_xor(hashed, lax.shift_right_logical(hashed, jnp.int32(16)))
    return hashed


CHUNKS = 4
TABLE_ROWS = 64


def front_kernel(
    shards, cols,
    base_ref, in_ref, gr_ref, low_in_ref, low_gr_ref, table_ref,
    pair, mine, land, full, block, sends, recvs, sends_z, recvs_z, sends_g, recvs_g, sends_x, recvs_x,
    store,
):
    me = lax.axis_index("proj")
    rest = shards // 2
    x, z = lax.rem(me, 2), me // 2
    rows = in_ref.shape[0] // 2
    half = rows // 2
    piece = half // rest
    parts = [in_ref, gr_ref]
    partner = z * 2 + (1 - x)
    others = [lax.rem(z + d, rest) for d in range(1, rest)]

    barrier = pltpu.get_barrier_semaphore()
    for target in [partner] + [o * 2 + x for o in others]:
        pl.semaphore_signal(
            barrier, inc=1, device_id={"proj": target}, device_id_type=pl.DeviceIdType.MESH
        )
    pl.semaphore_wait(barrier, rest)

    def remote(src, dst, send, recv, target):
        return pltpu.make_async_remote_copy(
            src_ref=src, dst_ref=dst, send_sem=send, recv_sem=recv,
            device_id={"proj": target}, device_id_type=pl.DeviceIdType.MESH,
        )

    def span(start, size):
        return pl.ds(pl.multiple_of(start, 16), size)

    one, two, three, four = {}, {}, {}, {}
    for c in range(CHUNKS):
        r0 = (c % 2) * rows
        one[c] = remote(
            parts[c // 2].at[span(r0 + (1 - x) * half, half)], pair.at[c],
            sends.at[c], recvs.at[c], partner,
        )
        one[c].start()

    def stage1(c):
        r0 = (c % 2) * rows
        one[c].wait_recv()
        mine[c] = (
            parts[c // 2][span(r0 + x * half, half), :].astype(jnp.float32)
            + pair[c].astype(jnp.float32)
        ).astype(jnp.bfloat16)
        two[c] = []
        for d in range(1, rest):
            s = c * (rest - 1) + d - 1
            copy = remote(
                mine.at[c, span(others[d - 1] * piece, piece)], land.at[s],
                sends_z.at[s], recvs_z.at[s], others[d - 1] * 2 + x,
            )
            copy.start()
            two[c].append(copy)

    def stage2(c):
        total = mine[c, span(z * piece, piece), :].astype(jnp.float32)
        for copy in two[c]:
            copy.wait_recv()
        for d in range(1, rest):
            total = total + land[c * (rest - 1) + d - 1].astype(jnp.float32)
        where = span((c % 2) * rows + x * half + z * piece, piece)
        full[c // 2, where, :] = (UPDATE_MULTIPLIER * total).astype(jnp.bfloat16)
        three[c] = []
        for d in range(1, rest):
            s = c * (rest - 1) + d - 1
            copy = remote(
                full.at[c // 2, where], full.at[c // 2, where],
                sends_g.at[s], recvs_g.at[s], others[d - 1] * 2 + x,
            )
            copy.start()
            three[c].append(copy)

    def stage3(c):
        for copy in three[c]:
            copy.wait_recv()
        where = span((c % 2) * rows + x * half, half)
        four[c] = remote(
            full.at[c // 2, where], full.at[c // 2, where], sends_x.at[c], recvs_x.at[c], partner
        )
        four[c].start()

    blocks = table_ref.shape[0] // TABLE_ROWS
    step, wide = 16, 512
    local = lax.broadcasted_iota(jnp.int32, (step, wide), 0) * cols + lax.broadcasted_iota(
        jnp.int32, (step, wide), 1
    )
    per_tile = 128 // TABLE_ROWS

    def stored(b):
        slot = lax.rem(b, 2)
        return pltpu.make_async_copy(
            block.at[slot],
            table_ref.at[pl.ds(pl.multiple_of(b * TABLE_ROWS, TABLE_ROWS), TABLE_ROWS)],
            store.at[slot],
        )

    def table_block(b, carry):
        slot = lax.rem(b, 2)

        @pl.when(b >= 2)
        def _():
            stored(b - 2).wait()

        base = base_ref[b // per_tile] + lax.rem(b, per_tile) * (TABLE_ROWS * cols)

        def piece_rows(i, inner):
            row = lax.rem(i, TABLE_ROWS // step) * step
            left = (i // (TABLE_ROWS // step)) * (4 * wide)
            for j in range(4):
                h = local + (base + row * cols + left + j * wide)
                h = h ^ lax.shift_right_logical(h, jnp.int32(16))
                h = h * jnp.int32(M1)
                h = h ^ lax.shift_right_logical(h, jnp.int32(15))
                h = h * jnp.int32(M2_UP)
                h = h ^ lax.shift_left(h, jnp.int32(16))
                sign = jnp.where(h < 0, jnp.float32(-1.0), jnp.float32(1.0))
                block[
                    slot,
                    pl.ds(pl.multiple_of(row, step), step),
                    pl.ds(pl.multiple_of(left + j * wide, wide), wide),
                ] = sign.astype(jnp.bfloat16)
            return inner

        lax.fori_loop(0, (TABLE_ROWS // step) * (cols // (4 * wide)), piece_rows, 0)
        stored(b).start()
        return carry

    plan = [
        [],
        [(stage1, 0)],
        [(stage1, 1)],
        [(stage2, 0), (stage1, 2)],
        [(stage2, 1), (stage1, 3)],
        [(stage3, 0), (stage2, 2)],
        [(stage3, 1), (stage2, 3), (stage3, 2), (stage3, 3)],
    ]
    ticks = len(plan) - 1
    for t, jobs in enumerate(plan):
        for job, c in jobs:
            job(c)
        if t < ticks:
            lax.fori_loop(blocks * t // ticks, blocks * (t + 1) // ticks, table_block, 0)
    for c in range(CHUNKS):
        four[c].wait_recv()
    low_in_ref[...] = full[0]
    low_gr_ref[...] = full[1]
    stored(blocks - 2).wait()
    stored(blocks - 1).wait()
    for c in range(CHUNKS):
        for copy in [one[c], four[c]] + two[c] + three[c]:
            copy.wait_send()


def front(bases, part_in, part_gr, shards, cols):
    total, rank = part_in.shape
    rest = shards // 2
    half = total // 4
    vmem = pl.BlockSpec(memory_space=pltpu.VMEM)
    sems = [pltpu.SemaphoreType.DMA((CHUNKS,))] * 2
    many = [pltpu.SemaphoreType.DMA((CHUNKS * (rest - 1),))] * 4
    return pl.pallas_call(
        functools.partial(front_kernel, shards, cols),
        in_specs=[pl.BlockSpec(memory_space=pltpu.SMEM), vmem, vmem],
        out_specs=[vmem, vmem, pl.BlockSpec(memory_space=pl.ANY)],
        out_shape=[
            jax.ShapeDtypeStruct((total, rank), jnp.bfloat16),
            jax.ShapeDtypeStruct((total, rank), jnp.bfloat16),
            jax.ShapeDtypeStruct((bases.shape[0] * 128, cols), jnp.bfloat16),
        ],
        scratch_shapes=[
            pltpu.VMEM((CHUNKS, half, rank), jnp.bfloat16),
            pltpu.VMEM((CHUNKS, half, rank), jnp.bfloat16),
            pltpu.VMEM((CHUNKS * (rest - 1), half // rest, rank), jnp.bfloat16),
            pltpu.VMEM((2, total, rank), jnp.bfloat16),
            pltpu.VMEM((2, TABLE_ROWS, cols), jnp.bfloat16),
        ] + sems + many + sems + [pltpu.SemaphoreType.DMA((2,))],
        compiler_params=pltpu.CompilerParams(
            collective_id=1, has_side_effects=True, vmem_limit_bytes=40 * 1024 * 1024
        ),
        name="front",
    )(bases, part_in, part_gr)


def step_kernel(wide_ref, low_ref, moment_ref, second_ref, order_ref, out_ref):
    grad = lax.dot_general(
        low_ref[0], wide_ref[0], (((0,), (0,)), ((), ())), preferred_element_type=jnp.float32
    )
    out_ref[...] = (
        (0.9 * moment_ref[...] + 0.1 * grad)
        * lax.rsqrt(0.999 * second_ref[...] + 0.001 * grad * grad)
    ).astype(jnp.bfloat16)


def steps(wide, low, moment, second, after, name):
    n, tok, w = wide.shape
    whole = pl.BlockSpec((RANK, w), lambda i: (0, 0))
    return pl.pallas_call(
        step_kernel,
        grid=(n,),
        in_specs=[
            pl.BlockSpec((1, tok, w), lambda i: (i, 0, 0)),
            pl.BlockSpec((1, tok, RANK), lambda i: (i, 0, 0)),
            whole,
            whole,
            pl.BlockSpec(memory_space=pl.ANY),
        ],
        out_specs=pl.BlockSpec((RANK, w), lambda i: (i, 0)),
        out_shape=jax.ShapeDtypeStruct((n * RANK, w), jnp.bfloat16),
        cost_estimate=pl.CostEstimate(
            flops=n * tok * w * RANK * 2, bytes_accessed=n * tok * w * 2, transcendentals=0
        ),
        compiler_params=pltpu.CompilerParams(vmem_limit_bytes=32 * 1024 * 1024),
        name=name,
    )(wide, low, moment, second, after)


def project_kernel(has_prior, *refs):
    if has_prior:
        step_ref, table_ref, side_ref, prior_ref, out_ref = refs
    else:
        step_ref, table_ref, side_ref, out_ref = refs
    n = step_ref.shape[0] // RANK
    mixed = jnp.dot(step_ref[...], table_ref[...], preferred_element_type=jnp.float32)
    side = side_ref[...].astype(jnp.float32)
    for i in range(n):
        row = jnp.sum(mixed[i * RANK : (i + 1) * RANK] * side, axis=0, keepdims=True)
        if has_prior:
            row = row + prior_ref[i : i + 1, :]
        out_ref[i : i + 1, :] = row


def project(step, tables, which, name, prior):
    rows, w = step.shape
    n = rows // RANK
    cols = tables.shape[1]
    tile = min(512, w)
    inner = w // tile
    edge = 2 * w // RANK
    out = pl.BlockSpec((None, n, tile), lambda k: (k // inner, 0, k % inner))
    in_specs = [
        pl.BlockSpec((rows, w), lambda k: (0, 0)),
        pl.BlockSpec((w, tile), lambda k: (which, k)),
        pl.BlockSpec((RANK, tile), lambda k: (edge + which, k)),
    ]
    operands = [step, tables, tables]
    if prior is not None:
        in_specs.append(out)
        operands.append(prior)
    return pl.pallas_call(
        functools.partial(project_kernel, prior is not None),
        grid=(cols // tile,),
        in_specs=in_specs,
        out_specs=out,
        out_shape=jax.ShapeDtypeStruct((cols // w, n, w), jnp.float32),
        cost_estimate=pl.CostEstimate(
            flops=2 * rows * w * cols, bytes_accessed=2 * w * cols + 2 * rows * w, transcendentals=0
        ),
        compiler_params=pltpu.CompilerParams(vmem_limit_bytes=40 * 1024 * 1024),
        name=name,
    )(*operands)


def finish_kernel(
    shards, langs, nval,
    proj_ref, val_ref, hot_ref, square_ref, count_ref,
    feat_ref, score_ref,
    land, message, notes, send1, recv1, send2, recv2,
):
    me = lax.axis_index("proj")
    n, w = feat_ref.shape
    cols = shards * w
    barrier = pltpu.get_barrier_semaphore()
    for d in range(1, shards):
        pl.semaphore_signal(
            barrier, inc=1, device_id={"proj": lax.rem(me + d, shards)},
            device_id_type=pl.DeviceIdType.MESH,
        )
    pl.semaphore_wait(barrier, shards - 1)

    first = []
    for d in range(1, shards):
        target = lax.rem(me + d, shards)
        copy = pltpu.make_async_remote_copy(
            src_ref=proj_ref.at[target], dst_ref=land.at[d - 1],
            send_sem=send1.at[d - 1], recv_sem=recv1.at[d - 1],
            device_id={"proj": target}, device_id_type=pl.DeviceIdType.MESH,
        )
        copy.start()
        first.append(copy)
    message[n:, :] = jnp.zeros((message.shape[0] - n, message.shape[1]), jnp.float32)
    message[16 : 16 + n, :nval] = square_ref[...]
    raw = proj_ref[me]
    for copy in first:
        copy.wait_recv()
    for d in range(1, shards):
        raw = raw + land[d - 1]
    dots = lax.dot_general(
        raw.astype(jnp.bfloat16), val_ref[...], (((1,), (1,)), ((), ())),
        preferred_element_type=jnp.float32,
    )
    own = jnp.zeros((n, nval), jnp.float32)
    for l in range(langs):
        own = own + hot_ref[:, l : l + 1] * dots[:, l * nval : (l + 1) * nval]
    message[:n, :nval] = own
    message[:n, nval:] = jnp.broadcast_to(
        jnp.sum(raw * raw, axis=1, keepdims=True), (n, message.shape[1] - nval)
    )
    second = []
    for d in range(1, shards):
        target = lax.rem(me + d, shards)
        copy = pltpu.make_async_remote_copy(
            src_ref=message, dst_ref=notes.at[d - 1],
            send_sem=send2.at[d - 1], recv_sem=recv2.at[d - 1],
            device_id={"proj": target}, device_id_type=pl.DeviceIdType.MESH,
        )
        copy.start()
        second.append(copy)
    total = message[...]
    for copy in second:
        copy.wait_recv()
    for d in range(1, shards):
        total = total + notes[d - 1]
    inverse = lax.rsqrt(total[:n, nval : nval + 1] / cols + 1e-06)
    feat_ref[...] = raw * inverse
    rms = jnp.sqrt(total[16 : 16 + n, :nval] / cols + 1e-06)
    similar = total[:n, :nval] * inverse / (math.sqrt(cols) * rms)
    live = lax.broadcasted_iota(jnp.int32, (n, nval), 1) < count_ref[...]
    best = jnp.max(jnp.where(live, similar, jnp.float32(-1e30)), axis=1, keepdims=True)
    score_ref[...] = jnp.broadcast_to(best, score_ref.shape)
    for copy in first + second:
        copy.wait_send()


def finish(projected, all_val, hot, own_square, count):
    shards, n, w = projected.shape
    langs, nval = all_val.shape[0], all_val.shape[1]
    vmem = pl.BlockSpec(memory_space=pltpu.VMEM)
    return pl.pallas_call(
        functools.partial(finish_kernel, shards, langs, nval),
        in_specs=[vmem] * 5,
        out_specs=[vmem] * 2,
        out_shape=[
            jax.ShapeDtypeStruct((n, w), jnp.float32),
            jax.ShapeDtypeStruct((n, 128), jnp.float32),
        ],
        scratch_shapes=[
            pltpu.VMEM((shards - 1, n, w), jnp.float32),
            pltpu.VMEM((32, nval + 128), jnp.float32),
            pltpu.VMEM((shards - 1, 32, nval + 128), jnp.float32),
            pltpu.SemaphoreType.DMA((shards - 1,)),
            pltpu.SemaphoreType.DMA((shards - 1,)),
            pltpu.SemaphoreType.DMA((shards - 1,)),
            pltpu.SemaphoreType.DMA((shards - 1,)),
        ],
        compiler_params=pltpu.CompilerParams(
            collective_id=0, has_side_effects=True, vmem_limit_bytes=32 * 1024 * 1024
        ),
        name="finish",
    )(projected, all_val.reshape(langs * nval, w), hot, own_square, count)


def per_device(
    mapped_layer_arguments,
    loss_slope_at_result,
    left_lowrank_weights,
    right_lowrank_weights,
    mean_estimate_left,
    variance_estimate_left,
    mean_estimate_right,
    variance_estimate_right,
    heldout_sketched_slopes,
    tongue_label_per_example,
    heldout_example_tally,
    sketch_random_key,
):
    shard_id = lax.axis_index("proj")
    shards = lax.axis_size("proj")
    n, tok, w = mapped_layer_arguments.shape
    K = w * shards

    part_in = jnp.einsum(
        "ntw,wr->ntr", mapped_layer_arguments, left_lowrank_weights,
        preferred_element_type=jnp.float32,
    ).astype(jnp.bfloat16)
    part_gr = jnp.einsum(
        "ntw,rw->ntr", loss_slope_at_result, right_lowrank_weights,
        preferred_element_type=jnp.float32,
    ).astype(jnp.bfloat16)

    seed4 = sketch_random_key[0] * 4
    inner = jnp.arange(w // RANK, dtype=jnp.int32) * (RANK * K) + shard_id * (w * K)
    bases = jnp.concatenate([
        scramble(seed4 + 1) + inner,
        scramble(seed4 + 2) + inner,
        scramble(seed4)[None],
        scramble(seed4 + 3)[None],
    ])
    low_in, low_gr, tables = front(
        bases, part_in.reshape(n * tok, RANK), part_gr.reshape(n * tok, RANK), shards, K
    )
    low_in = low_in.reshape(n, tok, RANK)
    low_gr = low_gr.reshape(n, tok, RANK)

    up = steps(
        loss_slope_at_result, low_in, mean_estimate_right, variance_estimate_right, tables,
        "steps_up"
    )
    half = project(up, tables, 0, "project_up", None)
    dn = steps(
        mapped_layer_arguments, low_gr, mean_estimate_left.T, variance_estimate_left.T, half,
        "steps_down"
    )
    projected = project(dn, tables, 1, "project_down", half)

    all_val = lax.all_gather(heldout_sketched_slopes, "lang", axis=0, tiled=True)
    val_wide = all_val.astype(jnp.float32)
    val_square = jnp.sum(val_wide * val_wide, axis=-1)
    lang_of = tongue_label_per_example[:, 0]
    num_langs = heldout_example_tally.shape[0]
    hot = (lang_of[:, None] == lax.iota(jnp.int32, num_langs)[None, :]).astype(jnp.float32)
    own_square = jnp.sum(hot[:, :, None] * val_square[None, :, :], axis=1)
    count_own = jnp.sum(
        hot.astype(jnp.int32) * heldout_example_tally[None, :], axis=1, keepdims=True
    )
    features, scores = finish(projected, all_val, hot, own_square, count_own)
    scores = scores[:, 0]
    return (features, scores)


def solution(mesh):
    in_specs = (
        P("lang", None, "proj"),
        P("lang", None, "proj"),
        P("proj", None),
        P(None, "proj"),
        P("proj", None),
        P("proj", None),
        P(None, "proj"),
        P(None, "proj"),
        P("lang", None, "proj"),
        P("lang", None),
        P(),
        P(),
    )
    out_specs = (P("lang", "proj"), P("lang"))
    return jax.shard_map(
        per_device, mesh=mesh, in_specs=in_specs, out_specs=out_specs, check_vma=False
    )
```

```python
import functools
import math

import jax
import jax.numpy as jnp
from jax import lax
from jax.experimental import pallas as pl
from jax.experimental.pallas import tpu as pltpu
from jax.sharding import PartitionSpec as P

RANK = 128
UPDATE_MULTIPLIER = 1.25
M1 = 2146121005
M2_UP = (739982445 * 4 + 2**31) % 2**32 - 2**31


def scramble(hashed):
    hashed = jnp.bitwise_xor(hashed, lax.shift_right_logical(hashed, jnp.int32(16)))
    hashed = hashed * 2146121005
    hashed = jnp.bitwise_xor(hashed, lax.shift_right_logical(hashed, jnp.int32(15)))
    hashed = hashed * 739982445
    hashed = jnp.bitwise_xor(hashed, lax.shift_right_logical(hashed, jnp.int32(16)))
    return hashed


CHUNKS = 4
TABLE_ROWS = 64


def front_kernel(
    shards, cols,
    base_ref, in_ref, gr_ref, low_in_ref, low_gr_ref, table_ref,
    pair, mine, land, full, block, sends, recvs, sends_z, recvs_z, sends_g, recvs_g, sends_x, recvs_x,
    store,
):
    me = lax.axis_index("proj")
    rest = shards // 2
    x, z = lax.rem(me, 2), me // 2
    rows = in_ref.shape[0] // 2
    half = rows // 2
    piece = half // rest
    parts = [in_ref, gr_ref]
    partner = z * 2 + (1 - x)
    others = [lax.rem(z + d, rest) for d in range(1, rest)]

    barrier = pltpu.get_barrier_semaphore()
    for target in [partner] + [o * 2 + x for o in others]:
        pl.semaphore_signal(
            barrier, inc=1, device_id={"proj": target}, device_id_type=pl.DeviceIdType.MESH
        )
    pl.semaphore_wait(barrier, rest)

    def remote(src, dst, send, recv, target):
        return pltpu.make_async_remote_copy(
            src_ref=src, dst_ref=dst, send_sem=send, recv_sem=recv,
            device_id={"proj": target}, device_id_type=pl.DeviceIdType.MESH,
        )

    def span(start, size):
        return pl.ds(pl.multiple_of(start, 16), size)

    one, two, three, four = {}, {}, {}, {}
    for c in range(CHUNKS):
        r0 = (c % 2) * rows
        one[c] = remote(
            parts[c // 2].at[span(r0 + (1 - x) * half, half)], pair.at[c],
            sends.at[c], recvs.at[c], partner,
        )
        one[c].start()

    def stage1(c):
        r0 = (c % 2) * rows
        one[c].wait_recv()
        mine[c] = (
            parts[c // 2][span(r0 + x * half, half), :].astype(jnp.float32)
            + pair[c].astype(jnp.float32)
        ).astype(jnp.bfloat16)
        two[c] = []
        for d in range(1, rest):
            s = c * (rest - 1) + d - 1
            copy = remote(
                mine.at[c, span(others[d - 1] * piece, piece)], land.at[s],
                sends_z.at[s], recvs_z.at[s], others[d - 1] * 2 + x,
            )
            copy.start()
            two[c].append(copy)

    def stage2(c):
        total = mine[c, span(z * piece, piece), :].astype(jnp.float32)
        for copy in two[c]:
            copy.wait_recv()
        for d in range(1, rest):
            total = total + land[c * (rest - 1) + d - 1].astype(jnp.float32)
        where = span((c % 2) * rows + x * half + z * piece, piece)
        full[c // 2, where, :] = (UPDATE_MULTIPLIER * total).astype(jnp.bfloat16)
        three[c] = []
        for d in range(1, rest):
            s = c * (rest - 1) + d - 1
            copy = remote(
                full.at[c // 2, where], full.at[c // 2, where],
                sends_g.at[s], recvs_g.at[s], others[d - 1] * 2 + x,
            )
            copy.start()
            three[c].append(copy)

    def stage3(c):
        for copy in three[c]:
            copy.wait_recv()
        where = span((c % 2) * rows + x * half, half)
        four[c] = remote(
            full.at[c // 2, where], full.at[c // 2, where], sends_x.at[c], recvs_x.at[c], partner
        )
        four[c].start()

    blocks = table_ref.shape[0] // TABLE_ROWS
    step, wide = 16, 512
    local = lax.broadcasted_iota(jnp.int32, (step, wide), 0) * cols + lax.broadcasted_iota(
        jnp.int32, (step, wide), 1
    )
    per_tile = 128 // TABLE_ROWS

    def stored(b):
        slot = lax.rem(b, 2)
        return pltpu.make_async_copy(
            block.at[slot],
            table_ref.at[pl.ds(pl.multiple_of(b * TABLE_ROWS, TABLE_ROWS), TABLE_ROWS)],
            store.at[slot],
        )

    def table_block(b, carry):
        slot = lax.rem(b, 2)

        @pl.when(b >= 2)
        def _():
            stored(b - 2).wait()

        base = base_ref[b // per_tile] + lax.rem(b, per_tile) * (TABLE_ROWS * cols)

        def piece_rows(i, inner):
            row = lax.rem(i, TABLE_ROWS // step) * step
            left = (i // (TABLE_ROWS // step)) * (4 * wide)
            for j in range(4):
                h = local + (base + row * cols + left + j * wide)
                h = h ^ lax.shift_right_logical(h, jnp.int32(16))
                h = h * jnp.int32(M1)
                h = h ^ lax.shift_right_logical(h, jnp.int32(15))
                h = h * jnp.int32(M2_UP)
                h = h ^ lax.shift_left(h, jnp.int32(16))
                sign = jnp.where(h < 0, jnp.float32(-1.0), jnp.float32(1.0))
                block[
                    slot,
                    pl.ds(pl.multiple_of(row, step), step),
                    pl.ds(pl.multiple_of(left + j * wide, wide), wide),
                ] = sign.astype(jnp.bfloat16)
            return inner

        lax.fori_loop(0, (TABLE_ROWS // step) * (cols // (4 * wide)), piece_rows, 0)
        stored(b).start()
        return carry

    plan = [
        [],
        [(stage1, 0)],
        [(stage1, 1)],
        [(stage2, 0), (stage1, 2)],
        [(stage2, 1), (stage1, 3)],
        [(stage3, 0), (stage2, 2)],
        [(stage3, 1), (stage2, 3), (stage3, 2), (stage3, 3)],
    ]
    ticks = len(plan) - 1
    for t, jobs in enumerate(plan):
        for job, c in jobs:
            job(c)
        if t < ticks:
            lax.fori_loop(blocks * t // ticks, blocks * (t + 1) // ticks, table_block, 0)
    for c in range(CHUNKS):
        four[c].wait_recv()
    low_in_ref[...] = full[0]
    low_gr_ref[...] = full[1]
    stored(blocks - 2).wait()
    stored(blocks - 1).wait()
    for c in range(CHUNKS):
        for copy in [one[c], four[c]] + two[c] + three[c]:
            copy.wait_send()


def front(bases, part_in, part_gr, shards, cols):
    total, rank = part_in.shape
    rest = shards // 2
    half = total // 4
    vmem = pl.BlockSpec(memory_space=pltpu.VMEM)
    sems = [pltpu.SemaphoreType.DMA((CHUNKS,))] * 2
    many = [pltpu.SemaphoreType.DMA((CHUNKS * (rest - 1),))] * 4
    return pl.pallas_call(
        functools.partial(front_kernel, shards, cols),
        in_specs=[pl.BlockSpec(memory_space=pltpu.SMEM), vmem, vmem],
        out_specs=[vmem, vmem, pl.BlockSpec(memory_space=pl.ANY)],
        out_shape=[
            jax.ShapeDtypeStruct((total, rank), jnp.bfloat16),
            jax.ShapeDtypeStruct((total, rank), jnp.bfloat16),
            jax.ShapeDtypeStruct((bases.shape[0] * 128, cols), jnp.bfloat16),
        ],
        scratch_shapes=[
            pltpu.VMEM((CHUNKS, half, rank), jnp.bfloat16),
            pltpu.VMEM((CHUNKS, half, rank), jnp.bfloat16),
            pltpu.VMEM((CHUNKS * (rest - 1), half // rest, rank), jnp.bfloat16),
            pltpu.VMEM((2, total, rank), jnp.bfloat16),
            pltpu.VMEM((2, TABLE_ROWS, cols), jnp.bfloat16),
        ] + sems + many + sems + [pltpu.SemaphoreType.DMA((2,))],
        compiler_params=pltpu.CompilerParams(
            collective_id=1, has_side_effects=True, vmem_limit_bytes=24 * 1024 * 1024
        ),
        name="front",
    )(bases, part_in, part_gr)


def step_kernel(wide_ref, low_ref, moment_ref, second_ref, order_ref, out_ref):
    grad = lax.dot_general(
        low_ref[0], wide_ref[0], (((0,), (0,)), ((), ())), preferred_element_type=jnp.float32
    )
    out_ref[...] = (
        (0.9 * moment_ref[...] + 0.1 * grad)
        * lax.rsqrt(0.999 * second_ref[...] + 0.001 * grad * grad)
    ).astype(jnp.bfloat16)


def steps(wide, low, moment, second, after, name):
    n, tok, w = wide.shape
    whole = pl.BlockSpec((RANK, w), lambda i: (0, 0))
    return pl.pallas_call(
        step_kernel,
        grid=(n,),
        in_specs=[
            pl.BlockSpec((1, tok, w), lambda i: (i, 0, 0)),
            pl.BlockSpec((1, tok, RANK), lambda i: (i, 0, 0)),
            whole,
            whole,
            pl.BlockSpec(memory_space=pl.ANY),
        ],
        out_specs=pl.BlockSpec((RANK, w), lambda i: (i, 0)),
        out_shape=jax.ShapeDtypeStruct((n * RANK, w), jnp.bfloat16),
        cost_estimate=pl.CostEstimate(
            flops=n * tok * w * RANK * 2, bytes_accessed=n * tok * w * 2, transcendentals=0
        ),
        compiler_params=pltpu.CompilerParams(vmem_limit_bytes=32 * 1024 * 1024),
        name=name,
    )(wide, low, moment, second, after)


def project_kernel(has_prior, *refs):
    if has_prior:
        step_ref, table_ref, side_ref, prior_ref, out_ref = refs
    else:
        step_ref, table_ref, side_ref, out_ref = refs
    n = step_ref.shape[0] // RANK
    mixed = jnp.dot(step_ref[...], table_ref[...], preferred_element_type=jnp.float32)
    side = side_ref[...].astype(jnp.float32)
    for i in range(n):
        row = jnp.sum(mixed[i * RANK : (i + 1) * RANK] * side, axis=0, keepdims=True)
        if has_prior:
            row = row + prior_ref[i : i + 1, :]
        out_ref[i : i + 1, :] = row


def project(step, tables, which, name, prior):
    rows, w = step.shape
    n = rows // RANK
    cols = tables.shape[1]
    tile = min(512, w)
    inner = w // tile
    edge = 2 * w // RANK
    out = pl.BlockSpec((None, n, tile), lambda k: (k // inner, 0, k % inner))
    in_specs = [
        pl.BlockSpec((rows, w), lambda k: (0, 0)),
        pl.BlockSpec((w, tile), lambda k: (which, k)),
        pl.BlockSpec((RANK, tile), lambda k: (edge + which, k)),
    ]
    operands = [step, tables, tables]
    if prior is not None:
        in_specs.append(out)
        operands.append(prior)
    return pl.pallas_call(
        functools.partial(project_kernel, prior is not None),
        grid=(cols // tile,),
        in_specs=in_specs,
        out_specs=out,
        out_shape=jax.ShapeDtypeStruct((cols // w, n, w), jnp.float32),
        cost_estimate=pl.CostEstimate(
            flops=2 * rows * w * cols, bytes_accessed=2 * w * cols + 2 * rows * w, transcendentals=0
        ),
        compiler_params=pltpu.CompilerParams(vmem_limit_bytes=40 * 1024 * 1024),
        name=name,
    )(*operands)


def finish_kernel(
    shards, langs, nval,
    proj_ref, val_ref, hot_ref, square_ref, count_ref,
    feat_ref, score_ref,
    land, message, notes, send1, recv1, send2, recv2,
):
    me = lax.axis_index("proj")
    n, w = feat_ref.shape
    cols = shards * w
    barrier = pltpu.get_barrier_semaphore()
    for d in range(1, shards):
        pl.semaphore_signal(
            barrier, inc=1, device_id={"proj": lax.rem(me + d, shards)},
            device_id_type=pl.DeviceIdType.MESH,
        )
    pl.semaphore_wait(barrier, shards - 1)

    first = []
    for d in range(1, shards):
        target = lax.rem(me + d, shards)
        copy = pltpu.make_async_remote_copy(
            src_ref=proj_ref.at[target], dst_ref=land.at[d - 1],
            send_sem=send1.at[d - 1], recv_sem=recv1.at[d - 1],
            device_id={"proj": target}, device_id_type=pl.DeviceIdType.MESH,
        )
        copy.start()
        first.append(copy)
    message[...] = jnp.zeros(message.shape, jnp.bfloat16)
    message[16 : 16 + n, :nval] = square_ref[...].astype(jnp.bfloat16)
    raw = proj_ref[me]
    for copy in first:
        copy.wait_recv()
    for d in range(1, shards):
        raw = raw + land[d - 1]
    dots = lax.dot_general(
        raw.astype(jnp.bfloat16), val_ref[...], (((1,), (1,)), ((), ())),
        preferred_element_type=jnp.float32,
    )
    own = jnp.zeros((n, nval), jnp.float32)
    for l in range(langs):
        own = own + hot_ref[:, l : l + 1] * dots[:, l * nval : (l + 1) * nval]
    message[:n, :nval] = own.astype(jnp.bfloat16)
    message[:n, nval:] = jnp.broadcast_to(
        jnp.sum(raw * raw, axis=1, keepdims=True), (n, message.shape[1] - nval)
    ).astype(jnp.bfloat16)
    second = []
    for d in range(1, shards):
        target = lax.rem(me + d, shards)
        copy = pltpu.make_async_remote_copy(
            src_ref=message, dst_ref=notes.at[d - 1],
            send_sem=send2.at[d - 1], recv_sem=recv2.at[d - 1],
            device_id={"proj": target}, device_id_type=pl.DeviceIdType.MESH,
        )
        copy.start()
        second.append(copy)
    total = message[...].astype(jnp.float32)
    for copy in second:
        copy.wait_recv()
    for d in range(1, shards):
        total = total + notes[d - 1].astype(jnp.float32)
    inverse = lax.rsqrt(total[:n, nval : nval + 1] / cols + 1e-06)
    feat_ref[...] = raw * inverse
    rms = jnp.sqrt(total[16 : 16 + n, :nval] / cols + 1e-06)
    similar = total[:n, :nval] * inverse / (math.sqrt(cols) * rms)
    live = lax.broadcasted_iota(jnp.int32, (n, nval), 1) < count_ref[...]
    best = jnp.max(jnp.where(live, similar, jnp.float32(-1e30)), axis=1, keepdims=True)
    score_ref[...] = jnp.broadcast_to(best, score_ref.shape)
    for copy in first + second:
        copy.wait_send()


def finish(projected, all_val, hot, own_square, count):
    shards, n, w = projected.shape
    langs, nval = all_val.shape[0], all_val.shape[1]
    vmem = pl.BlockSpec(memory_space=pltpu.VMEM)
    return pl.pallas_call(
        functools.partial(finish_kernel, shards, langs, nval),
        in_specs=[vmem] * 5,
        out_specs=[vmem] * 2,
        out_shape=[
            jax.ShapeDtypeStruct((n, w), jnp.float32),
            jax.ShapeDtypeStruct((n, 128), jnp.float32),
        ],
        scratch_shapes=[
            pltpu.VMEM((shards - 1, n, w), jnp.float32),
            pltpu.VMEM((32, nval + 128), jnp.bfloat16),
            pltpu.VMEM((shards - 1, 32, nval + 128), jnp.bfloat16),
            pltpu.SemaphoreType.DMA((shards - 1,)),
            pltpu.SemaphoreType.DMA((shards - 1,)),
            pltpu.SemaphoreType.DMA((shards - 1,)),
            pltpu.SemaphoreType.DMA((shards - 1,)),
        ],
        compiler_params=pltpu.CompilerParams(
            collective_id=0, has_side_effects=True, vmem_limit_bytes=32 * 1024 * 1024
        ),
        name="finish",
    )(projected, all_val.reshape(langs * nval, w), hot, own_square, count)


def per_device(
    mapped_layer_arguments,
    loss_slope_at_result,
    left_lowrank_weights,
    right_lowrank_weights,
    mean_estimate_left,
    variance_estimate_left,
    mean_estimate_right,
    variance_estimate_right,
    heldout_sketched_slopes,
    tongue_label_per_example,
    heldout_example_tally,
    sketch_random_key,
):
    shard_id = lax.axis_index("proj")
    shards = lax.axis_size("proj")
    n, tok, w = mapped_layer_arguments.shape
    K = w * shards

    part_in = jnp.einsum(
        "ntw,wr->ntr", mapped_layer_arguments, left_lowrank_weights,
        preferred_element_type=jnp.float32,
    ).astype(jnp.bfloat16)
    part_gr = jnp.einsum(
        "ntw,rw->ntr", loss_slope_at_result, right_lowrank_weights,
        preferred_element_type=jnp.float32,
    ).astype(jnp.bfloat16)

    seed4 = sketch_random_key[0] * 4
    inner = jnp.arange(w // RANK, dtype=jnp.int32) * (RANK * K) + shard_id * (w * K)
    bases = jnp.concatenate([
        scramble(seed4 + 1) + inner,
        scramble(seed4 + 2) + inner,
        scramble(seed4)[None],
        scramble(seed4 + 3)[None],
    ])
    low_in, low_gr, tables = front(
        bases, part_in.reshape(n * tok, RANK), part_gr.reshape(n * tok, RANK), shards, K
    )
    low_in = low_in.reshape(n, tok, RANK)
    low_gr = low_gr.reshape(n, tok, RANK)

    up = steps(
        loss_slope_at_result, low_in, mean_estimate_right, variance_estimate_right, tables,
        "steps_up"
    )
    half = project(up, tables, 0, "project_up", None)
    dn = steps(
        mapped_layer_arguments, low_gr, mean_estimate_left.T, variance_estimate_left.T, half,
        "steps_down"
    )
    projected = project(dn, tables, 1, "project_down", half)

    all_val = lax.all_gather(heldout_sketched_slopes, "lang", axis=0, tiled=True)
    val_wide = all_val.astype(jnp.float32)
    val_square = jnp.sum(val_wide * val_wide, axis=-1)
    lang_of = tongue_label_per_example[:, 0]
    num_langs = heldout_example_tally.shape[0]
    hot = (lang_of[:, None] == lax.iota(jnp.int32, num_langs)[None, :]).astype(jnp.float32)
    own_square = jnp.sum(hot[:, :, None] * val_square[None, :, :], axis=1)
    count_own = jnp.sum(
        hot.astype(jnp.int32) * heldout_example_tally[None, :], axis=1, keepdims=True
    )
    features, scores = finish(projected, all_val, hot, own_square, count_own)
    scores = scores[:, 0]
    return (features, scores)


def solution(mesh):
    in_specs = (
        P("lang", None, "proj"),
        P("lang", None, "proj"),
        P("proj", None),
        P(None, "proj"),
        P("proj", None),
        P("proj", None),
        P(None, "proj"),
        P(None, "proj"),
        P("lang", None, "proj"),
        P("lang", None),
        P(),
        P(),
    )
    out_specs = (P("lang", "proj"), P("lang"))
    return jax.shard_map(
        per_device, mesh=mesh, in_specs=in_specs, out_specs=out_specs, check_vma=False
    )
```
